32 devices in a mesh: ctx: 4 (over y, x), head: 8 (over z, core).
Axes of the slice: x: 2, y: 2, z: 4, core: 2. Of those that a mesh axis runs over, the one named last changes fastest.
Arguments:
- queries: bfloat16 [1024, 64, 128], P('ctx', 'head'), may hold values from -2 to 2
- keys: bfloat16 [1024, 64, 128], P('ctx', 'head'), may hold values from -2 to 2
- values: bfloat16 [1024, 64, 128], P('ctx', 'head'), may hold values from -2 to 2
- out_weight: bfloat16 [8192, 6144], P('head'), may hold values from -0.0625 to 0.0625
- decay_rate: float32 [64], P('head'), may hold values from 1.953125e-05 to 0.04
- out_grad: bfloat16 [1024, 6144], P(('ctx', 'head')), may hold values from -4 to 4
Outputs:
- layer_out: bfloat16 [1024, 6144], P(('ctx', 'head'))
- query_grad: bfloat16 [1024, 64, 128], P('ctx', 'head')
- key_grad: bfloat16 [1024, 64, 128], P('ctx', 'head')
- value_grad: bfloat16 [1024, 64, 128], P('ctx', 'head')
- weight_grad: float32 [8192, 6144], P('head', 'ctx')
The draws below stay inside these ranges and needn't reach their ends.
All inputs are finite; a program needn't handle non-finite values.
Results may differ from the reference program's by a relative error of at most 0.0057.
Values may be sent and summed in bfloat16 or wider, within the bound.
A program may use at most 128 MiB of HBM per device.

```python
import math
import jax
import jax.numpy as jnp
from jax import lax

D = 6144
HEADS = 64
DH = 128
TOK_DEV = 256
TOKENS = 1024
N_CTX = 4


def strengthened(drawn, stream_key, source, target, shards_of, factor):
    owner, partner = [(jnp.arange(drawn.shape[axis_at]) // (drawn.shape[axis_at] // shards_of)).reshape([-1 if axis == axis_at else 1 for axis in range(drawn.ndim)]) for axis_at in (source, target)]
    chosen = jax.random.permutation(stream_key, shards_of)[partner]
    strong = (owner == chosen) | (owner == (partner + shards_of // 2) % shards_of)
    return jnp.where(strong, factor * drawn, drawn)


def shard_levels(rng, dims, cuts, least, top_value):
    loudness, own = 1.0, jax.random.fold_in(rng, 6)
    for axis_at, blocks in cuts:
        heights = jnp.exp(jax.random.uniform(jax.random.fold_in(own, axis_at), (blocks,), jnp.float32, least / len(cuts), top_value / len(cuts)))
        loudness = loudness * jnp.repeat(heights, dims[axis_at] // blocks).reshape([-1 if axis == axis_at else 1 for axis in range(len(dims))])
    return loudness


def gaussian(key, extent, width, reach, cuts=(), held_as=jnp.bfloat16):
    result = width * jax.random.normal(key, extent, jnp.float32)
    if cuts:
        result = result * shard_levels(key, extent, cuts, -0.22, 0.18)
    return jnp.clip(result, -reach, reach).astype(held_as)


def bell_draw_with(stream_key, dims, width, most, pieces, heavy, kind=jnp.bfloat16):
    entries = width * jax.random.normal(stream_key, dims, jnp.float32)
    if pieces:
        entries = entries * shard_levels(stream_key, dims, pieces, -0.22, 0.18)
    return jnp.clip(strengthened(entries, jax.random.fold_in(stream_key, 3), *heavy), -most, most).astype(kind)


def setup_inputs(seed: int = 0) -> dict:
    splits = jax.random.split(jax.random.key(seed), 7)
    queries = gaussian(splits[0], (TOKENS, HEADS, DH), (1.0 / (DH * TOKENS) ** 0.1667), 2.0, ((0, 4), (1, 8)))
    keys = gaussian(splits[1], (TOKENS, HEADS, DH), (1.0 / (DH * TOKENS) ** 0.1667), 2.0, ((0, 4), (1, 8)))
    values = gaussian(splits[2], (TOKENS, HEADS, DH), (1.0 / (DH * TOKENS) ** 0.1667), 2.0, ((0, 4), (1, 8)))
    out_weight = gaussian(splits[3], (HEADS * DH, D), (HEADS * DH) ** -0.5, 0.0625, ((0, 8),))
    decay_rate = jnp.clip(jnp.exp(math.log(0.04) - 7.624619 * jax.random.uniform(splits[4], (HEADS,), jnp.float32) ** shard_levels(splits[4], (HEADS,), ((0, 8),), -0.2, 0.2)), 1.9531249563442543e-05, 0.04)
    out_grad = bell_draw_with(splits[5], (TOKENS, D), (1.0 / (DH * TOKENS) ** 0.1667), 4.0, ((0, 32),), (0, 1, 32, 2.75))
    return {"queries": queries, "keys": keys, "values": values, "out_weight": out_weight, "decay_rate": decay_rate, "out_grad": out_grad}


precise_mode = lax.Precision.HIGHEST


def rounded(array):
    return lax.optimization_barrier(array.astype(jnp.bfloat16)).astype(jnp.float32)


def product(form, left, right):
    return jnp.einsum(form, left, right, precision=precise_mode)


def reference(queries, keys, values, out_weight, decay_rate, out_grad):
    places = jnp.arange(TOK_DEV, dtype=jnp.float32)
    offsets = places[:, None] - places[None, :]
    mask_decay = jnp.where(offsets[None] >= 0, jnp.exp(-decay_rate[:, None, None] * jnp.maximum(offsets, 0.0)[None]), 0.0)
    end_weight = jnp.exp(-decay_rate[None, :] * (TOK_DEV - 1.0 - places)[:, None])
    start_weight = jnp.exp(-decay_rate[None, :] * places[:, None])
    inner_weight = jnp.exp(-decay_rate[None, :] * (places + 1.0)[:, None])
    tail_weight = jnp.exp(-decay_rate[None, :] * (TOK_DEV - places)[:, None])
    block_factor = jnp.exp(-decay_rate * TOK_DEV)
    block_shape = (N_CTX, TOK_DEV, HEADS, DH)
    query_blocks = queries.reshape(block_shape)
    key_blocks = keys.reshape(block_shape)
    value_blocks = values.reshape(block_shape)

    def forward_block(prev_state, inputs):
        query_wide = inputs[0].astype(jnp.float32)
        key_wide = inputs[1].astype(jnp.float32)
        value_wide = inputs[2].astype(jnp.float32)
        attn = rounded(product("thd,shd->hts", query_wide, key_wide) * mask_decay)
        inside = product("hts,she->the", attn, value_wide)
        outside = inner_weight[:, :, None] * product("thd,hde->the", query_wide, prev_state)
        keys_end = rounded(key_wide * end_weight[:, :, None])
        block_state = product("thd,the->hde", keys_end, value_wide)
        next_state = block_factor[:, None, None] * prev_state + block_state
        return next_state, (rounded(inside + outside), prev_state)

    zero_state = jnp.zeros((HEADS, DH, DH), jnp.float32)
    _, (attn_blocks, prev_states) = lax.scan(forward_block, zero_state, (query_blocks, key_blocks, value_blocks))
    flat_out = attn_blocks.reshape(TOKENS, HEADS * DH).astype(jnp.bfloat16)
    layer_out = jnp.dot(flat_out, out_weight, preferred_element_type=jnp.float32).astype(jnp.bfloat16)
    grad_flat = jnp.dot(out_grad, out_weight.T, preferred_element_type=jnp.float32).astype(jnp.bfloat16)
    weight_grad = jnp.dot(flat_out.T, out_grad, preferred_element_type=jnp.float32)
    grad_blocks = grad_flat.reshape(block_shape)

    def backward_block(next_grad, inputs):
        query_wide = inputs[0].astype(jnp.float32)
        key_wide = inputs[1].astype(jnp.float32)
        value_wide = inputs[2].astype(jnp.float32)
        grad_wide = inputs[3].astype(jnp.float32)
        prev_state = inputs[4]
        attn = rounded(product("thd,shd->hts", query_wide, key_wide) * mask_decay)
        queries_start = rounded(query_wide * start_weight[:, :, None])
        grad_block = product("thd,the->hde", queries_start, grad_wide)
        grad_scores = rounded(product("the,she->hts", grad_wide, value_wide) * mask_decay)
        query_grad = product("hts,shd->thd", grad_scores, key_wide) + inner_weight[:, :, None] * product("the,hde->thd", grad_wide, prev_state)
        key_grad = product("hts,thd->shd", grad_scores, query_wide) + tail_weight[:, :, None] * product("she,hde->shd", value_wide, next_grad)
        value_grad = product("hts,the->she", attn, grad_wide) + tail_weight[:, :, None] * product("shd,hde->she", key_wide, next_grad)
        carried = block_factor[:, None, None] * next_grad + grad_block
        return carried, (query_grad.astype(jnp.bfloat16), key_grad.astype(jnp.bfloat16), value_grad.astype(jnp.bfloat16))

    _, (query_grads, key_grads, value_grads) = lax.scan(backward_block, zero_state, (query_blocks, key_blocks, value_blocks, grad_blocks, prev_states), reverse=True)
    full_shape = (TOKENS, HEADS, DH)
    return (layer_out, query_grads.reshape(full_shape), key_grads.reshape(full_shape), value_grads.reshape(full_shape), weight_grad)
```

```python
import jax
import jax.numpy as jnp
from jax import lax
from jax.sharding import PartitionSpec as P

F32 = jnp.float32
BF16 = jnp.bfloat16


def rounds(n):
    if n & (n - 1) == 0:
        return [(r, [(i, i ^ r) for i in range(n)]) for r in range(1, n)]
    return [(r, [(i, (i + r) % n) for i in range(n)]) for r in range(1, n)]


def target(me, r, n):
    return me ^ r if n & (n - 1) == 0 else (me + r) % n


def earlier_states(state, rate, length, n, sign):
    sent = state.astype(BF16)
    total = jnp.zeros(state.shape, F32)
    for r in range(1, n):
        pairs = [(i, i + r * sign) for i in range(n) if 0 <= i + r * sign < n]
        got = lax.ppermute(sent, "ctx", pairs).astype(F32)
        total = total + jnp.exp(-rate * float(length * (r - 1)))[:, None, None] * got
    return total


def make_body(mesh):
    n_ctx = mesh.shape["ctx"]

    def body(queries, keys, values, out_weight, decay_rate, out_grad):
        length, heads_here, head_size = queries.shape
        width = out_weight.shape[1]
        share = width // n_ctx
        me = lax.axis_index("ctx")
        piece = lax.all_gather(out_grad, "head", axis=0, tiled=True)

        places = jnp.arange(length, dtype=F32)
        offsets = places[:, None] - places[None, :]
        mask_decay = jnp.where(
            offsets[None] >= 0,
            jnp.exp(-decay_rate[:, None, None] * jnp.maximum(offsets, 0.0)[None]),
            0.0,
        )
        end_weight = jnp.exp(-decay_rate[:, None] * (length - 1.0 - places)[None, :])
        start_weight = jnp.exp(-decay_rate[:, None] * places[None, :])
        inner_weight = jnp.exp(-decay_rate[:, None] * (places + 1.0)[None, :])
        tail_weight = jnp.exp(-decay_rate[:, None] * (length - places)[None, :])

        q = jnp.swapaxes(queries, 0, 1)
        k = jnp.swapaxes(keys, 0, 1)
        v = jnp.swapaxes(values, 0, 1)

        def mm(form, a, b):
            return jnp.einsum(form, a, b, preferred_element_type=F32)

        keys_end = (k * end_weight[:, :, None]).astype(BF16)
        block_state = mm("htd,hte->hde", keys_end, v)
        prev_state = earlier_states(block_state, decay_rate, length, n_ctx, 1).astype(BF16)
        attn = (mm("htd,hsd->hts", q, k) * mask_decay).astype(BF16)
        inside = mm("hts,hse->hte", attn, v)
        outside = inner_weight[:, :, None] * mm("htd,hde->hte", q, prev_state)
        attn_out = (inside + outside).astype(BF16)
        flat_out = jnp.swapaxes(attn_out, 0, 1).reshape(length, heads_here * head_size)
        part = jnp.dot(flat_out, out_weight, preferred_element_type=F32).astype(BF16)
        layer_out = lax.psum_scatter(part, "head", scatter_dimension=0, tiled=True)

        grad_flat = lax.dot_general(
            piece, out_weight, (((1,), (1,)), ((), ())), preferred_element_type=F32
        ).astype(BF16)
        g = jnp.swapaxes(grad_flat.reshape(length, heads_here, head_size), 0, 1)
        queries_start = (q * start_weight[:, :, None]).astype(BF16)
        grad_block = mm("htd,hte->hde", queries_start, g)
        next_grad = earlier_states(grad_block, decay_rate, length, n_ctx, -1).astype(BF16)

        def columns(at):
            return lax.dynamic_slice_in_dim(piece, at * share, share, 1)

        def outer(a, b):
            return lax.dot_general(a, b, (((0,), (0,)), ((), ())), preferred_element_type=F32)

        weight_grad = outer(flat_out, columns(me))
        for r, pairs in rounds(n_ctx):
            their_out = lax.ppermute(flat_out, "ctx", pairs)
            their_grad = lax.ppermute(columns(target(me, r, n_ctx)), "ctx", pairs)
            weight_grad = weight_grad + outer(their_out, their_grad)

        grad_scores = (mm("hte,hse->hts", g, v) * mask_decay).astype(BF16)
        query_grad = mm("hts,hsd->htd", grad_scores, k) + inner_weight[:, :, None] * mm(
            "hte,hde->htd", g, prev_state
        )
        key_grad = mm("hts,htd->hsd", grad_scores, q) + tail_weight[:, :, None] * mm(
            "hse,hde->hsd", v, next_grad
        )
        value_grad = mm("hts,hte->hse", attn, g) + tail_weight[:, :, None] * mm(
            "hsd,hde->hse", k, next_grad
        )

        def back(x):
            return jnp.swapaxes(x.astype(BF16), 0, 1)

        return layer_out, back(query_grad), back(key_grad), back(value_grad), weight_grad

    return body


def solution(mesh):
    return jax.shard_map(
        make_body(mesh),
        mesh=mesh,
        in_specs=(
            P("ctx", "head", None),
            P("ctx", "head", None),
            P("ctx", "head", None),
            P("head", None),
            P("head"),
            P(("ctx", "head"), None),
        ),
        out_specs=(
            P(("ctx", "head"), None),
            P("ctx", "head", None),
            P("ctx", "head", None),
            P("ctx", "head", None),
            P("head", "ctx"),
        ),
        check_vma=False,
    )
```

```python
import jax
import jax.numpy as jnp
from jax import lax
from jax.sharding import PartitionSpec as P

F32 = jnp.float32
BF16 = jnp.bfloat16


def rounds(n):
    if n & (n - 1) == 0:
        return [(r, [(i, i ^ r) for i in range(n)]) for r in range(1, n)]
    return [(r, [(i, (i + r) % n) for i in range(n)]) for r in range(1, n)]


def target(me, r, n):
    return me ^ r if n & (n - 1) == 0 else (me + r) % n


def earlier_states(state, rate, length, n, sign):
    sent = state.astype(BF16)
    total = jnp.zeros(state.shape, F32)
    for r in range(1, n):
        pairs = [(i, i + r * sign) for i in range(n) if 0 <= i + r * sign < n]
        got = lax.ppermute(sent, "ctx", pairs).astype(F32)
        total = total + jnp.exp(-rate * float(length * (r - 1)))[:, None, None] * got
    return total


def make_body(mesh):
    n_ctx = mesh.shape["ctx"]
    n_head = mesh.shape["head"]
    cores = 2 if n_head % 2 == 0 else 1
    n_z = n_head // cores
    swap = [(h, h ^ 1) for h in range(n_head)]

    def other_core(x):
        return lax.ppermute(x, "head", swap)

    z_rounds = [
        (r, [(a * cores + c, b * cores + c) for a, b in pairs for c in range(cores)])
        for r, pairs in rounds(n_z)
    ]

    def source(me, r, n):
        return me ^ r if n & (n - 1) == 0 else (me - r + n) % n

    def body(queries, keys, values, out_weight, decay_rate, out_grad):
        length, heads_here, head_size = queries.shape
        width = out_weight.shape[1]
        share = width // n_ctx
        rows = out_grad.shape[0]
        half = rows * n_z
        me = lax.axis_index("ctx")
        head_at = lax.axis_index("head")
        z, core = head_at // cores, head_at % cores

        arrived = [lax.ppermute(out_grad, "head", pairs) for _, pairs in z_rounds]

        def own_first(x):
            x = jnp.moveaxis(x.reshape(n_z, cores, rows, x.shape[1]), 1, 0)
            x = jnp.where(core == 0, x, x[::-1])
            return [x[0].reshape(half, -1), x[1].reshape(half, -1)]

        places = jnp.arange(length, dtype=F32)
        offsets = places[:, None] - places[None, :]
        mask_decay = jnp.where(
            offsets[None] >= 0,
            jnp.exp(-decay_rate[:, None, None] * jnp.maximum(offsets, 0.0)[None]),
            0.0,
        )
        end_weight = jnp.exp(-decay_rate[:, None] * (length - 1.0 - places)[None, :])
        start_weight = jnp.exp(-decay_rate[:, None] * places[None, :])
        inner_weight = jnp.exp(-decay_rate[:, None] * (places + 1.0)[None, :])
        tail_weight = jnp.exp(-decay_rate[:, None] * (length - places)[None, :])

        q = jnp.swapaxes(queries, 0, 1)
        k = jnp.swapaxes(keys, 0, 1)
        v = jnp.swapaxes(values, 0, 1)

        def mm(form, a, b):
            return jnp.einsum(form, a, b, preferred_element_type=F32)

        keys_end = (k * end_weight[:, :, None]).astype(BF16)
        block_state = mm("htd,hte->hde", keys_end, v)
        prev_state = earlier_states(block_state, decay_rate, length, n_ctx, 1).astype(BF16)
        attn = (mm("htd,hsd->hts", q, k) * mask_decay).astype(BF16)
        inside = mm("hts,hse->hte", attn, v)
        outside = inner_weight[:, :, None] * mm("htd,hde->hte", q, prev_state)
        attn_out = (inside + outside).astype(BF16)
        flat_out = jnp.swapaxes(attn_out, 0, 1).reshape(length, heads_here * head_size)
        flat_own, flat_other = own_first(flat_out)

        sent = jnp.dot(flat_other, out_weight, preferred_element_type=F32).astype(BF16)
        total = jnp.dot(flat_own, out_weight, preferred_element_type=F32)
        total, arrived = lax.optimization_barrier((total, arrived))

        held = jnp.zeros((n_z, rows, width), BF16)
        held = lax.dynamic_update_slice_in_dim(held, out_grad[None], z, 0)
        for (r, _), got in zip(z_rounds, arrived):
            held = lax.dynamic_update_slice_in_dim(held, got[None], source(z, r, n_z), 0)
        held = held.reshape(half, width)

        def columns(x, at):
            return lax.dynamic_slice_in_dim(x, at * share, share, 1)

        ctx_rounds = rounds(n_ctx)
        near = [
            lax.ppermute(columns(held, target(me, r, n_ctx)), "ctx", pairs)
            for r, pairs in ctx_rounds
        ]
        halves = [held, other_core(held)]

        total = (total + other_core(sent)).reshape(n_z, rows, width)

        def rows_of(at):
            return lax.dynamic_index_in_dim(total, at, 0, keepdims=False)

        layer_out = rows_of(z)
        for r, pairs in z_rounds:
            got = lax.ppermute(rows_of(target(z, r, n_z)).astype(BF16), "head", pairs)
            layer_out = layer_out + got
        layer_out = layer_out.astype(BF16)

        both = jnp.concatenate(halves, 0)
        grad_flat = lax.dot_general(
            both, out_weight, (((1,), (1,)), ((), ())), preferred_element_type=F32
        ).astype(BF16)
        g = grad_flat.reshape(cores, n_z, rows, heads_here, head_size)
        g = jnp.where(core == 0, g, g[::-1])
        g = jnp.transpose(g, (3, 1, 0, 2, 4)).reshape(heads_here, length, head_size)
        queries_start = (q * start_weight[:, :, None]).astype(BF16)
        grad_block = mm("htd,hte->hde", queries_start, g)
        next_grad = earlier_states(grad_block, decay_rate, length, n_ctx, -1).astype(BF16)

        def outer(a, b):
            return lax.dot_general(a, b, (((0,), (0,)), ((), ())), preferred_element_type=F32)

        flat = jnp.concatenate([flat_own, flat_other], 0)
        theirs = [lax.ppermute(flat, "ctx", pairs) for _, pairs in ctx_rounds]
        weight_grad = outer(flat, columns(both, me))
        grad_scores = (mm("hte,hse->hts", g, v) * mask_decay).astype(BF16)
        query_grad = mm("hts,hsd->htd", grad_scores, k) + inner_weight[:, :, None] * mm(
            "hte,hde->htd", g, prev_state
        )
        query_grad = query_grad.astype(BF16)
        query_grad, near, theirs = lax.optimization_barrier((query_grad, near, theirs))
        near = jnp.concatenate(near, 0)
        far = other_core(near)
        weight_grad = weight_grad + outer(jnp.concatenate([x[:half] for x in theirs], 0), near)
        weight_grad = weight_grad + outer(jnp.concatenate([x[half:] for x in theirs], 0), far)
        key_grad = mm("hts,htd->hsd", grad_scores, q) + tail_weight[:, :, None] * mm(
            "hse,hde->hsd", v, next_grad
        )
        value_grad = mm("hts,hte->hse", attn, g) + tail_weight[:, :, None] * mm(
            "hsd,hde->hse", k, next_grad
        )

        def back(x):
            return jnp.swapaxes(x.astype(BF16), 0, 1)

        return layer_out, back(query_grad), back(key_grad), back(value_grad), weight_grad

    return body


def solution(mesh):
    return jax.shard_map(
        make_body(mesh),
        mesh=mesh,
        in_specs=(
            P("ctx", "head", None),
            P("ctx", "head", None),
            P("ctx", "head", None),
            P("head", None),
            P("head"),
            P(("ctx", "head"), None),
        ),
        out_specs=(
            P(("ctx", "head"), None),
            P("ctx", "head", None),
            P("ctx", "head", None),
            P("ctx", "head", None),
            P("head", "ctx"),
        ),
        check_vma=False,
    )
```

```python
import functools

import jax
import jax.numpy as jnp
from jax import lax
from jax.experimental import pallas as pl
from jax.experimental.pallas import tpu as pltpu
from jax.sharding import PartitionSpec as P

F32 = jnp.float32
BF16 = jnp.bfloat16


def rounds(n):
    if n & (n - 1) == 0:
        return [(r, [(i, i ^ r) for i in range(n)]) for r in range(1, n)]
    return [(r, [(i, (i + r) % n) for i in range(n)]) for r in range(1, n)]


def target(me, r, n):
    return me ^ r if n & (n - 1) == 0 else (me + r) % n


def sent_states(state, n, sign):
    return [
        lax.ppermute(state, "ctx", [(i, i + r * sign) for i in range(n) if 0 <= i + r * sign < n])
        for r in range(1, n)
    ]


def mm(a, b, at, bt):
    return lax.dot_general(a, b, (((at,), (bt,)), ((), ())), preferred_element_type=F32)


def mask_of(rate, length):
    rows = lax.broadcasted_iota(jnp.int32, (length, length), 0)
    cols = lax.broadcasted_iota(jnp.int32, (length, length), 1)
    gap = (rows - cols).astype(F32)
    return jnp.where(gap >= 0, jnp.exp(-rate * jnp.maximum(gap, 0.0)), 0.0)


def falling(rate, length, size):
    rows = lax.broadcasted_iota(jnp.int32, (length, size), 0).astype(F32)
    return lambda first, slope: jnp.exp(-rate * (first + slope * rows))


def folded(refs, j, rate, length):
    total = refs[0][j].astype(F32)
    for r, ref in enumerate(refs[1:]):
        total = total + jnp.exp(jnp.full(total.shape, -rate * (length * (r + 1.0)))) * ref[j].astype(F32)
    return total


def two_terms(x):
    high = x.astype(BF16)
    return high, (x - high.astype(F32)).astype(BF16)


def forward_kernel(cores, rows, n_got, rate_ref, core_ref, q_ref, k_ref, v_ref, *refs):
    got, (flat_ref, attn_ref, prev_ref) = refs[:n_got], refs[n_got:]
    length, size = q_ref.shape[1:]
    rate = rate_ref[pl.program_id(0)]
    q, k, v = q_ref[0], k_ref[0], v_ref[0]
    attn = (mm(q, k, 1, 1) * mask_of(rate, length)).astype(BF16)
    attn_ref[0] = attn
    prev = folded(got, 0, rate, length)
    prev_ref[0] = prev
    high, low = two_terms(prev)
    outside = falling(rate, length, size)(1.0, 1.0) * (mm(q, high, 1, 0) + mm(q, low, 1, 0))
    out = (mm(attn, v, 1, 0) + outside).astype(BF16)
    half = length // cores
    for c in range(cores):
        base = pl.multiple_of(jnp.where(core_ref[0] == c, 0, half), half)
        for z in range(half // rows):
            at = (z * cores + c) * rows
            flat_ref[pl.ds(base + z * rows, rows), :] = out[at : at + rows]


def first_kernel(cores, rows, group, rate_ref, core_ref, own_ref, other_ref, w_ref, q_ref, k_ref, v_ref,
                 prev_ref, g_ref, block_ref, scores_ref, query_ref, both):
    length, size = q_ref.shape[1:]
    step = pl.program_id(0)

    @pl.when(step == 0)
    def _():
        half = length // cores
        for z in range(half // rows):
            for c in range(cores):
                ref = own_ref if c == 0 else other_ref
                place = c if cores == 1 else jnp.where(c == 0, core_ref[0], 1 - core_ref[0])
                at = pl.multiple_of((z * cores + place) * rows, rows)
                both[pl.ds(at, rows), :] = ref[z * rows : (z + 1) * rows, :]

    grads = mm(both[...], w_ref[...], 1, 1).astype(BF16)
    for j in range(group):
        rate = rate_ref[step * group + j]
        q, k, v = q_ref[j], k_ref[j], v_ref[j]
        g = grads[:, j * size : (j + 1) * size]
        g_ref[j] = g
        falls = falling(rate, length, size)
        start = (q.astype(F32) * falls(0.0, 1.0)).astype(BF16)
        block_ref[j] = mm(start, g, 0, 0).astype(BF16)
        scores = (mm(g, v, 1, 1) * mask_of(rate, length)).astype(BF16)
        scores_ref[j] = scores
        high, low = two_terms(prev_ref[j])
        outside = falls(1.0, 1.0) * (mm(g, high, 1, 1) + mm(g, low, 1, 1))
        query_ref[j] = (mm(scores, k, 1, 0) + outside).astype(BF16)


def second_kernel(n_got, rate_ref, q_ref, k_ref, v_ref, g_ref, attn_ref, scores_ref, *refs):
    got, (key_ref, value_ref) = refs[:n_got], refs[n_got:]
    length, size = q_ref.shape[1:]
    rate = rate_ref[pl.program_id(0)]
    tail = falling(rate, length, size)(float(length), -1.0)
    high, low = two_terms(folded(got, 0, rate, length))
    v, k = v_ref[0], k_ref[0]
    key_outside = tail * (mm(v, high, 1, 1) + mm(v, low, 1, 1))
    key_ref[0] = (mm(scores_ref[0], q_ref[0], 0, 0) + key_outside).astype(BF16)
    value_outside = tail * (mm(k, high, 1, 0) + mm(k, low, 1, 0))
    value_ref[0] = (mm(attn_ref[0], g_ref[0], 0, 0) + value_outside).astype(BF16)


SMEM = pl.BlockSpec(memory_space=pltpu.SMEM)


def per_head(*dims, group=1):
    return pl.BlockSpec((group, *dims), lambda i: (i, 0, 0))


def call(kernel, name, grid, in_specs, outs, out_specs, flops, bytes_accessed, scratch=()):
    return pl.pallas_call(
        kernel,
        name=name,
        grid=(grid,),
        in_specs=in_specs,
        out_shape=[jax.ShapeDtypeStruct(dims, kind) for dims, kind in outs],
        out_specs=out_specs,
        scratch_shapes=list(scratch),
        compiler_params=pltpu.CompilerParams(vmem_limit_bytes=40 * 1024 * 1024),
        cost_estimate=pl.CostEstimate(flops=flops, bytes_accessed=bytes_accessed, transcendentals=0),
    )


def make_body(mesh):
    n_ctx = mesh.shape["ctx"]
    n_head = mesh.shape["head"]
    cores = 2 if n_head % 2 == 0 else 1
    n_z = n_head // cores
    swap = [(h, h ^ 1) for h in range(n_head)]

    def other_core(x):
        return lax.ppermute(x, "head", swap)

    z_rounds = [
        (r, [(a * cores + c, b * cores + c) for a, b in pairs for c in range(cores)])
        for r, pairs in rounds(n_z)
    ]

    def source(me, r, n):
        return me ^ r if n & (n - 1) == 0 else (me - r + n) % n

    def body(queries, keys, values, out_weight, decay_rate, out_grad):
        length, heads_here, head_size = queries.shape
        width = out_weight.shape[1]
        share = width // n_ctx
        rows = out_grad.shape[0]
        half = rows * n_z
        me = lax.axis_index("ctx")
        head_at = lax.axis_index("head")
        z, core = head_at // cores, head_at % cores

        arrived = [lax.ppermute(out_grad, "head", pairs) for _, pairs in z_rounds]

        places = jnp.arange(length, dtype=F32)
        end_weight = jnp.exp(-decay_rate[:, None] * (length - 1.0 - places)[None, :])
        q = jnp.swapaxes(queries, 0, 1)
        k = jnp.swapaxes(keys, 0, 1)
        v = jnp.swapaxes(values, 0, 1)
        keys_end = (k * end_weight[:, :, None]).astype(BF16)
        block_state = jnp.einsum("htd,hte->hde", keys_end, v, preferred_element_type=F32)
        got = sent_states(block_state.astype(BF16), n_ctx, 1)
        core_at = jnp.reshape(core, (1,)).astype(jnp.int32)
        line = per_head(length, head_size)
        square = per_head(length, length)
        state = per_head(head_size, head_size)
        lines = (heads_here, length, head_size)
        squares = (heads_here, length, length)
        states = (heads_here, head_size, head_size)
        work = 2 * heads_here * length * length * head_size
        flat, attn, prev_state = call(
            functools.partial(forward_kernel, cores, rows, len(got)),
            "forward",
            heads_here,
            [SMEM, SMEM, line, line, line] + [state] * len(got),
            [((length, heads_here * head_size), BF16), (squares, BF16), (states, F32)],
            [pl.BlockSpec((length, head_size), lambda i: (0, i)), square, state],
            4 * work,
            8 * heads_here * length * length,
        )(decay_rate, core_at, q, k, v, *got)

        part = jnp.dot(flat, out_weight, preferred_element_type=F32).astype(BF16)
        part, arrived = lax.optimization_barrier((part, arrived))
        sent = part[half:]

        held = jnp.zeros((n_z, rows, width), BF16)
        held = lax.dynamic_update_slice_in_dim(held, out_grad[None], z, 0)
        for (r, _), got in zip(z_rounds, arrived):
            held = lax.dynamic_update_slice_in_dim(held, got[None], source(z, r, n_z), 0)
        held = held.reshape(half, width)

        def columns(x, at):
            return lax.dynamic_slice_in_dim(x, at * share, share, 1)

        ctx_rounds = rounds(n_ctx)
        near = [
            lax.ppermute(columns(held, target(me, r, n_ctx)), "ctx", pairs)
            for r, pairs in ctx_rounds
        ]
        halves = [held, other_core(held)]

        total = (part[:half].astype(F32) + other_core(sent)).reshape(n_z, rows, width)

        def rows_of(at):
            return lax.dynamic_index_in_dim(total, at, 0, keepdims=False)

        layer_out = rows_of(z)
        for r, pairs in z_rounds:
            got = lax.ppermute(rows_of(target(z, r, n_z)).astype(BF16), "head", pairs)
            layer_out = layer_out + got
        layer_out = layer_out.astype(BF16)

        group = 2 if heads_here % 2 == 0 else 1
        pair = per_head(length, head_size, group=group)
        pair_state = per_head(head_size, head_size, group=group)
        whole = pl.BlockSpec((half, width), lambda i: (0, 0))
        g, grad_block, grad_scores, query_grad = call(
            functools.partial(first_kernel, cores, rows, group),
            "backward_first",
            heads_here // group,
            [SMEM, SMEM, whole, whole, pl.BlockSpec((group * head_size, width), lambda i: (i, 0)),
             pair, pair, pair, pair_state],
            [(lines, BF16), (states, BF16), (squares, BF16), (lines, BF16)],
            [pair, pair_state, per_head(length, length, group=group), pair],
            4 * work + 2 * length * width * heads_here * head_size,
            2 * width * heads_here * head_size,
            [pltpu.VMEM((length, width), BF16)],
        )(decay_rate, core_at, halves[0], halves[-1], out_weight, q, k, v, prev_state)
        got = sent_states(grad_block, n_ctx, -1)
        both = jnp.concatenate(halves[:cores], 0)

        def outer(a, b):
            return lax.dot_general(a, b, (((0,), (0,)), ((), ())), preferred_element_type=F32)

        theirs = [lax.ppermute(flat, "ctx", pairs) for _, pairs in ctx_rounds]
        weight_grad = outer(flat, columns(both, me))
        query_grad, near, theirs = lax.optimization_barrier((query_grad, near, theirs))
        near = jnp.concatenate(near, 0)
        far = other_core(near)
        weight_grad = weight_grad + outer(jnp.concatenate([x[:half] for x in theirs], 0), near)
        weight_grad = weight_grad + outer(jnp.concatenate([x[half:] for x in theirs], 0), far)
        key_grad, value_grad = call(
            functools.partial(second_kernel, len(got)),
            "backward_second",
            heads_here,
            [SMEM, line, line, line, line, square, square] + [state] * len(got),
            [(lines, BF16), (lines, BF16)],
            [line, line],
            4 * work,
            8 * heads_here * length * length,
        )(decay_rate, q, k, v, g, attn, grad_scores, *got)

        def back(x):
            return jnp.swapaxes(x, 0, 1)

        return layer_out, back(query_grad), back(key_grad), back(value_grad), weight_grad

    return body


def solution(mesh):
    return jax.shard_map(
        make_body(mesh),
        mesh=mesh,
        in_specs=(
            P("ctx", "head", None),
            P("ctx", "head", None),
            P("ctx", "head", None),
            P("head", None),
            P("head"),
            P(("ctx", "head"), None),
        ),
        out_specs=(
            P(("ctx", "head"), None),
            P("ctx", "head", None),
            P("ctx", "head", None),
            P("ctx", "head", None),
            P("head", "ctx"),
        ),
        check_vma=False,
    )
```

```python
import functools

import jax
import jax.numpy as jnp
from jax import lax
from jax.experimental import pallas as pl
from jax.experimental.pallas import tpu as pltpu
from jax.sharding import PartitionSpec as P


F32 = jnp.float32
BF16 = jnp.bfloat16


def rounds(n):
    if n & (n - 1) == 0:
        return [(r, [(i, i ^ r) for i in range(n)]) for r in range(1, n)]
    return [(r, [(i, (i + r) % n) for i in range(n)]) for r in range(1, n)]


def target(me, r, n):
    return me ^ r if n & (n - 1) == 0 else (me + r) % n


def sent_states(state, n, sign):
    return [
        lax.ppermute(state, "ctx", [(i, i + r * sign) for i in range(n) if 0 <= i + r * sign < n])
        for r in range(1, n)
    ]


def mm(a, b, at, bt):
    return lax.dot_general(a, b, (((at,), (bt,)), ((), ())), preferred_element_type=F32)


def mask_of(rate, length):
    rows = lax.broadcasted_iota(jnp.int32, (length, length), 0)
    cols = lax.broadcasted_iota(jnp.int32, (length, length), 1)
    gap = (rows - cols).astype(F32)
    return jnp.where(gap >= 0, jnp.exp(-rate * jnp.maximum(gap, 0.0)), 0.0)


def falling(rate, length, size):
    rows = lax.broadcasted_iota(jnp.int32, (length, size), 0).astype(F32)
    return lambda first, slope: jnp.exp(-rate * (first + slope * rows))


def folded(refs, j, rate, length):
    total = refs[0][j].astype(F32)
    for r, ref in enumerate(refs[1:]):
        total = total + jnp.exp(jnp.full(total.shape, -rate * (length * (r + 1.0)))) * ref[j].astype(F32)
    return total


def two_terms(x):
    high = x.astype(BF16)
    return high, (x - high.astype(F32)).astype(BF16)


def forward_kernel(cores, rows, n_got, rate_ref, core_ref, q_ref, k_ref, v_ref, *refs):
    got, (flat_ref, attn_ref, prev_ref) = refs[:n_got], refs[n_got:]
    length, size = q_ref.shape[1:]
    rate = rate_ref[pl.program_id(0)]
    q, k, v = q_ref[0], k_ref[0], v_ref[0]
    attn = (mm(q, k, 1, 1) * mask_of(rate, length)).astype(BF16)
    attn_ref[0] = attn
    prev = folded(got, 0, rate, length)
    prev_ref[0] = prev
    high, low = two_terms(prev)
    outside = falling(rate, length, size)(1.0, 1.0) * (mm(q, high, 1, 0) + mm(q, low, 1, 0))
    out = (mm(attn, v, 1, 0) + outside).astype(BF16)
    half = length // cores
    for c in range(cores):
        base = pl.multiple_of(jnp.where(core_ref[0] == c, 0, half), half)
        for z in range(half // rows):
            at = (z * cores + c) * rows
            flat_ref[pl.ds(base + z * rows, rows), :] = out[at : at + rows]


def first_kernel(cores, rows, group, rate_ref, core_ref, own_ref, other_ref, w_ref, q_ref, k_ref, v_ref,
                 prev_ref, g_ref, block_ref, scores_ref, query_ref, both):
    length, size = q_ref.shape[1:]
    step = pl.program_id(0)

    @pl.when(step == 0)
    def _():
        half = length // cores
        for z in range(half // rows):
            for c in range(cores):
                ref = own_ref if c == 0 else other_ref
                place = c if cores == 1 else jnp.where(c == 0, core_ref[0], 1 - core_ref[0])
                at = pl.multiple_of((z * cores + place) * rows, rows)
                both[pl.ds(at, rows), :] = ref[z * rows : (z + 1) * rows, :]

    grads = mm(both[...], w_ref[...], 1, 1).astype(BF16)
    for j in range(group):
        rate = rate_ref[step * group + j]
        q, k, v = q_ref[j], k_ref[j], v_ref[j]
        g = grads[:, j * size : (j + 1) * size]
        g_ref[j] = g
        falls = falling(rate, length, size)
        start = (q.astype(F32) * falls(0.0, 1.0)).astype(BF16)
        block_ref[j] = mm(start, g, 0, 0).astype(BF16)
        scores = (mm(g, v, 1, 1) * mask_of(rate, length)).astype(BF16)
        scores_ref[j] = scores
        high, low = two_terms(prev_ref[j])
        outside = falls(1.0, 1.0) * (mm(g, high, 1, 1) + mm(g, low, 1, 1))
        query_ref[j] = (mm(scores, k, 1, 0) + outside).astype(BF16)


def second_kernel(n_got, rate_ref, q_ref, k_ref, v_ref, g_ref, attn_ref, scores_ref, *refs):
    got, (key_ref, value_ref) = refs[:n_got], refs[n_got:]
    length, size = q_ref.shape[1:]
    rate = rate_ref[pl.program_id(0)]
    tail = falling(rate, length, size)(float(length), -1.0)
    high, low = two_terms(folded(got, 0, rate, length))
    v, k = v_ref[0], k_ref[0]
    key_outside = tail * (mm(v, high, 1, 1) + mm(v, low, 1, 1))
    key_ref[0] = (mm(scores_ref[0], q_ref[0], 0, 0) + key_outside).astype(BF16)
    value_outside = tail * (mm(k, high, 1, 0) + mm(k, low, 1, 0))
    value_ref[0] = (mm(attn_ref[0], g_ref[0], 0, 0) + value_outside).astype(BF16)


SMEM = pl.BlockSpec(memory_space=pltpu.SMEM)


def per_head(*dims, group=1):
    return pl.BlockSpec((group, *dims), lambda i: (i, 0, 0))


def call(kernel, grid, in_specs, outs, out_specs, flops, bytes_accessed, scratch=()):
    return pl.pallas_call(
        kernel,
        grid=(grid,),
        in_specs=in_specs,
        out_shape=[jax.ShapeDtypeStruct(dims, kind) for dims, kind in outs],
        out_specs=out_specs,
        scratch_shapes=list(scratch),
        compiler_params=pltpu.CompilerParams(vmem_limit_bytes=40 * 1024 * 1024),
        cost_estimate=pl.CostEstimate(flops=flops, bytes_accessed=bytes_accessed, transcendentals=0),
    )


def make_body(mesh):
    n_ctx = mesh.shape["ctx"]
    n_head = mesh.shape["head"]
    cores = 2 if n_head % 2 == 0 else 1
    n_z = n_head // cores
    swap = [(h, h ^ 1) for h in range(n_head)]

    def other_core(x):
        return lax.ppermute(x, "head", swap)

    z_rounds = [
        (r, [(a * cores + c, b * cores + c) for a, b in pairs for c in range(cores)])
        for r, pairs in rounds(n_z)
    ]

    def source(me, r, n):
        return me ^ r if n & (n - 1) == 0 else (me - r + n) % n

    def body(queries, keys, values, out_weight, decay_rate, out_grad):
        length, heads_here, head_size = queries.shape
        width = out_weight.shape[1]
        share = width // n_ctx
        rows = out_grad.shape[0]
        half = rows * n_z
        me = lax.axis_index("ctx")
        head_at = lax.axis_index("head")
        z, core = head_at // cores, head_at % cores

        ctx_rounds = rounds(n_ctx)
        arrived = [lax.ppermute(out_grad, "head", pairs) for _, pairs in z_rounds]

        places = jnp.arange(length, dtype=F32)
        end_weight = jnp.exp(-decay_rate[:, None] * (length - 1.0 - places)[None, :])
        q = jnp.swapaxes(queries, 0, 1)
        k = jnp.swapaxes(keys, 0, 1)
        v = jnp.swapaxes(values, 0, 1)
        keys_end = (k * end_weight[:, :, None]).astype(BF16)
        block_state = jnp.einsum("htd,hte->hde", keys_end, v, preferred_element_type=F32)
        got = sent_states(block_state.astype(BF16), n_ctx, 1)
        core_at = jnp.reshape(core, (1,)).astype(jnp.int32)
        line = per_head(length, head_size)
        square = per_head(length, length)
        state = per_head(head_size, head_size)
        lines = (heads_here, length, head_size)
        squares = (heads_here, length, length)
        states = (heads_here, head_size, head_size)
        work = 2 * heads_here * length * length * head_size
        flat, attn, prev_state = call(
            functools.partial(forward_kernel, cores, rows, len(got)),
            heads_here,
            [SMEM, SMEM, line, line, line] + [state] * len(got),
            [((length, heads_here * head_size), BF16), (squares, BF16), (states, F32)],
            [pl.BlockSpec((length, head_size), lambda i: (0, i)), square, state],
            4 * work,
            8 * heads_here * length * length,
        )(decay_rate, core_at, q, k, v, *got)

        theirs = []
        for _, pairs in ctx_rounds:
            theirs.append(lax.ppermute(flat, "ctx", pairs))
        part = jnp.dot(flat, out_weight, preferred_element_type=F32).astype(BF16)
        part, arrived = lax.optimization_barrier((part, arrived))
        sent = part[half:]

        held = jnp.zeros((n_z, rows, width), BF16)
        held = lax.dynamic_update_slice_in_dim(held, out_grad[None], z, 0)
        for (r, _), got in zip(z_rounds, arrived):
            held = lax.dynamic_update_slice_in_dim(held, got[None], source(z, r, n_z), 0)
        held = held.reshape(half, width)

        def columns(x, at):
            return lax.dynamic_slice_in_dim(x, at * share, share, 1)


        near = [
            lax.ppermute(columns(held, target(me, r, n_ctx)), "ctx", pairs)
            for r, pairs in ctx_rounds
        ]
        halves = [held, other_core(held)]

        total = (part[:half].astype(F32) + other_core(sent)).reshape(n_z, rows, width)

        def rows_of(at):
            return lax.dynamic_index_in_dim(total, at, 0, keepdims=False)

        layer_out = rows_of(z)
        for r, pairs in z_rounds:
            got = lax.ppermute(rows_of(target(z, r, n_z)).astype(BF16), "head", pairs)
            layer_out = layer_out + got
        layer_out = layer_out.astype(BF16)

        group = 2 if heads_here % 2 == 0 else 1
        pair = per_head(length, head_size, group=group)
        pair_state = per_head(head_size, head_size, group=group)
        whole = pl.BlockSpec((half, width), lambda i: (0, 0))
        g, grad_block, grad_scores, query_grad = call(
            functools.partial(first_kernel, cores, rows, group),
            heads_here // group,
            [SMEM, SMEM, whole, whole, pl.BlockSpec((group * head_size, width), lambda i: (i, 0)),
             pair, pair, pair, pair_state],
            [(lines, BF16), (states, BF16), (squares, BF16), (lines, BF16)],
            [pair, pair_state, per_head(length, length, group=group), pair],
            4 * work + 2 * length * width * heads_here * head_size,
            2 * width * heads_here * head_size,
            [pltpu.VMEM((length, width), BF16)],
        )(decay_rate, core_at, halves[0], halves[-1], out_weight, q, k, v, prev_state)
        got = sent_states(grad_block, n_ctx, -1)
        both = jnp.concatenate(halves[:cores], 0)

        def outer(a, b):
            return lax.dot_general(a, b, (((0,), (0,)), ((), ())), preferred_element_type=F32)

        weight_grad = outer(flat, columns(both, me))
        query_grad, near, theirs = lax.optimization_barrier((query_grad, near, theirs))
        near = jnp.concatenate(near, 0)
        far = other_core(near)
        weight_grad = weight_grad + outer(jnp.concatenate([x[:half] for x in theirs], 0), near)
        weight_grad = weight_grad + outer(jnp.concatenate([x[half:] for x in theirs], 0), far)
        key_grad, value_grad = call(
            functools.partial(second_kernel, len(got)),
            heads_here,
            [SMEM, line, line, line, line, square, square] + [state] * len(got),
            [(lines, BF16), (lines, BF16)],
            [line, line],
            4 * work,
            8 * heads_here * length * length,
        )(decay_rate, q, k, v, g, attn, grad_scores, *got)

        def back(x):
            return jnp.swapaxes(x, 0, 1)

        return layer_out, back(query_grad), back(key_grad), back(value_grad), weight_grad

    return body


def solution(mesh):
    return jax.shard_map(
        make_body(mesh),
        mesh=mesh,
        in_specs=(
            P("ctx", "head", None),
            P("ctx", "head", None),
            P("ctx", "head", None),
            P("head", None),
            P("head"),
            P(("ctx", "head"), None),
        ),
        out_specs=(
            P(("ctx", "head"), None),
            P("ctx", "head", None),
            P("ctx", "head", None),
            P("ctx", "head", None),
            P("head", "ctx"),
        ),
        check_vma=False,
    )
```
